32 devices in a mesh: section: 4 (over y, core), ep: 8 (over z, x).
Axes of the slice: x: 2, y: 2, z: 4, core: 2. Of those that a mesh axis runs over, the one named last changes fastest.
Arguments:
- rows_in: bfloat16 [4, 64, 7168], P(None, 'ep'), may hold values from -6 to 6
- routes: int32 [4, 4, 64, 2], P('section', None, 'ep'), may hold values from 0 to 3, all different within a row; in each aligned block of 8 rows (0 to 7, 8 to 15, ..., all dimensions but the last counted through in order) at most 4 rows name the same one
- hot_blocks: int32 [4], P('section'), may hold values from 0 to 15
- gains: float32 [4, 7168], P('section'), may hold values from 0.1 to 1.9
- router: bfloat16 [4, 7168, 4], P('section'), may hold values from -0.0625 to 0.0625
- w_gate: bfloat16 [4, 7168, 4096], P('section', None, 'ep'), may hold values from -0.0625 to 0.0625
- w_up: bfloat16 [4, 7168, 4096], P('section', None, 'ep'), may hold values from -0.0625 to 0.0625
- w_down: bfloat16 [4, 4096, 7168], P('section', 'ep'), may hold values from -0.1875 to 0.1875
Outputs:
- section_rows: bfloat16 [4, 4, 64, 7168], P('section', None, 'ep')
- relative_load: float32 [4, 8], P('section', 'ep')
The draws below stay inside these ranges and needn't reach their ends.
Inputs may be any that keep to these rules, and one draw needn't show every extreme that they name: `routes`: in every layer and micro-batch the 8 rows of one device name each expert at most 4 times.
All inputs are finite; a program needn't handle non-finite values.
Results may differ from the reference program's by a relative error of at most 0.025.
Values may be sent and summed in bfloat16 or wider, within the bound.
A program may use at most 128 MiB of HBM per device.

```python
import math
import jax
import jax.numpy as jnp
import numpy as np
from jax import lax

D = 7168
FFW = 1024
BLK = 256
TOP = 2
MICRO = 4
TOK_DEV = 8
CAP = 4
EXPERTS = 4
BLOCKS = 16
LAYERS = 4
TOKENS = 64
N_EP = 8


def touch_ends(result, key, least, top_value):
    longest = result.shape.index(max(result.shape))
    spots = []
    for shift in (0, 1):
        where = [jax.random.randint(jax.random.fold_in(key, axis), (), 0, length) for axis, length in enumerate(result.shape)]
        where[longest] = (where[longest] + shift) % result.shape[longest]
        spots.append(tuple(where))
    return result.at[spots[0]].set(least).at[spots[1]].set(top_value)


def level_of(own_key, extent, cuts, smallest, high):
    gain = 1.0
    for position, shards_of in cuts:
        draws = jax.random.uniform(jax.random.fold_in(jax.random.fold_in(own_key, 6), position), (shards_of,), jnp.float32, smallest / len(cuts), high / len(cuts))
        gain = gain * jnp.repeat(jnp.exp(draws), extent[position] // shards_of).reshape((-1,) + (1,) * (len(extent) - 1 - position))
    return gain


def deal_out(stream_key, own, number, rows, amount, top, limit, slope):
    ranking = jax.random.permutation(stream_key, amount)
    heavy_load, common = shares(amount, rows * top, limit, slope, True), shares(amount, rows * top, limit, slope, False)
    places = jnp.arange(amount)

    def named(lengths, turn):
        used = int((lengths > 0).sum())
        fixed = max(1, used // 4)
        moved = fixed + (places - fixed + turn * (used - fixed)) % max(1, amount - fixed)
        return jnp.zeros((amount,), jnp.int32).at[ranking[jnp.where(places < fixed, places, moved)]].set(jnp.asarray(lengths, jnp.int32))

    lengths = jnp.where(number % 4 == 0, named(heavy_load, number // 4), named(common, number - number // 4 - 1))
    mixed = jax.random.permutation(jax.random.fold_in(own, 3), amount)
    donor, sink = mixed[0:amount // 2 * 2:2], mixed[1:amount // 2 * 2:2]
    room = jnp.minimum(lengths[donor] - 1, limit - lengths[sink]) // 2
    room = jnp.where((donor == ranking[0]) | (sink == ranking[0]) | (lengths[sink] == 0), 0, jnp.maximum(room, 0))
    moved = jax.random.randint(jax.random.fold_in(own, 4), (amount // 2,), 0, 1 << 20) % (room + 1)
    lengths = lengths.at[donor].add(-moved).at[sink].add(moved)
    members = jnp.searchsorted(jnp.cumsum(lengths), jnp.arange(rows * top), side="right").astype(jnp.int32)
    table = members.reshape(top, rows).T
    table = table[jax.random.permutation(jax.random.fold_in(own, 1), rows)]
    turn = jax.random.randint(jax.random.fold_in(own, 2), (rows, 1), 0, top)
    return jnp.take_along_axis(table, (jnp.arange(top)[None, :] + turn) % top, axis=1)


def shares(number_of, total, bound, skew, full):
    weights = [(1 << 20) // math.isqrt(grade ** skew) + 1 for grade in range(1, number_of + 1)]
    largest = bound if full else min(bound, max(-(-total // number_of), total * weights[0] // sum(weights)))
    least = 1 if total - largest >= number_of - 1 else 0
    holding, spare = [largest] + [least] * (number_of - 1), total - largest - least * (number_of - 1)
    while spare > 0:
        candidates = [i for i in range(1, number_of) if holding[i] < largest] or [i for i in range(1, number_of) if holding[i] < bound]
        pool, left = sum([weights[i] for i in candidates]), spare
        for i in candidates:
            extra = min(bound - holding[i], max(1, left * weights[i] // pool), spare)
            holding[i] = holding[i] + extra
            spare = spare - extra
    return np.array(holding)


def scatter_about(stream_key, shape, deviation, most, split=(), kind=jnp.bfloat16):
    gain = level_of(stream_key, shape, split, -0.22, 0.18) if split else 1.0
    result = jax.random.normal(stream_key, shape, jnp.float32) * deviation * gain
    return jnp.minimum(jnp.maximum(result, -most), most).astype(kind)


def setup_inputs(seed: int = 0) -> dict:
    key_of = jax.random.split(jax.random.key(seed), 9)
    rows_in = scatter_about(key_of[0], (MICRO, TOKENS, D), 1.0, 6.0, ((1, 8),))
    routes_keys = jax.random.split(jax.random.fold_in(key_of[1], 1), LAYERS * MICRO * TOKENS // TOK_DEV)
    routes_turns = jax.random.permutation(jax.random.fold_in(key_of[1], 3), LAYERS * MICRO * TOKENS // TOK_DEV)
    routes = jax.vmap(lambda own, number: deal_out(jax.random.fold_in(key_of[1], 2), own, number, TOK_DEV, EXPERTS, TOP, CAP, 2))(routes_keys, routes_turns).reshape((LAYERS, MICRO, TOKENS, TOP))
    hot_blocks = touch_ends(jax.random.randint(key_of[2], (LAYERS,), 0, BLOCKS), jax.random.fold_in(key_of[2], 1), 0, BLOCKS - 1).astype(jnp.int32)
    gains = jnp.clip(1.0 + 0.18 * jax.random.normal(key_of[3], (LAYERS, D), jnp.float32), 0.1, 1.9)
    router = scatter_about(key_of[4], (LAYERS, D, EXPERTS), D ** -0.5, 0.0625, ((0, 4),))
    w_gate = scatter_about(key_of[5], (LAYERS, D, EXPERTS * FFW), D ** -0.5, 0.0625, ((0, 4), (2, 8)))
    w_up = scatter_about(key_of[6], (LAYERS, D, EXPERTS * FFW), D ** -0.5, 0.0625, ((0, 4), (2, 8)))
    w_down = scatter_about(key_of[7], (LAYERS, EXPERTS * FFW, D), FFW ** -0.5, 0.1875, ((0, 4), (1, 8)))
    return {"rows_in": rows_in, "routes": routes, "hot_blocks": hot_blocks, "gains": gains, "router": router, "w_gate": w_gate, "w_up": w_up, "w_down": w_down}


def apply_layer(rows, route_ids, hot_index, norm_gain, router_w, gate_w, up_w, down_w, down_float):
    rows_float = rows.astype(jnp.float32)
    mean_square = lax.optimization_barrier(jnp.mean(rows_float * rows_float, axis=-1, keepdims=True))
    normed = (rows_float * lax.rsqrt(mean_square + 1e-06) * norm_gain).astype(jnp.bfloat16)
    scores = jax.nn.sigmoid(jnp.dot(normed, router_w, preferred_element_type=jnp.float32))
    chosen = jnp.take_along_axis(scores, route_ids, axis=1)
    gate_weights = 2.5 * chosen / lax.optimization_barrier(jnp.sum(chosen, axis=1, keepdims=True))
    gate_value = jnp.dot(normed, gate_w, preferred_element_type=jnp.float32)
    up_value = jnp.dot(normed, up_w, preferred_element_type=jnp.float32)
    activation = (jax.nn.silu(gate_value) * up_value).astype(jnp.bfloat16)
    column_block = jnp.arange(EXPERTS * FFW, dtype=jnp.int32) // BLK
    home_act = jnp.where((column_block != hot_index)[None, :], activation, jnp.zeros_like(activation))
    token_count = rows.shape[0]
    home_part = jnp.einsum('tpc,pcd->tpd', home_act.reshape(token_count, N_EP, 2 * BLK).astype(jnp.float32), down_float)
    home_part = lax.optimization_barrier(home_part.astype(jnp.bfloat16)).astype(jnp.float32)
    halves = home_part.reshape(token_count, EXPERTS, 2, D)
    pair_sum = halves[:, :, 0, :] + halves[:, :, 1, :]
    hot_act = lax.dynamic_slice_in_dim(activation, (hot_index * BLK).astype(jnp.int32), BLK, 1)
    hot_down = lax.dynamic_slice_in_dim(down_w, (hot_index * BLK).astype(jnp.int32), BLK, 0)
    hot_part = jnp.dot(hot_act, hot_down, preferred_element_type=jnp.float32)
    hot_part = lax.optimization_barrier(hot_part.astype(jnp.bfloat16)).astype(jnp.float32)
    one_hot = (route_ids[:, :, None] == jnp.arange(EXPERTS, dtype=jnp.int32)[None, None, :]).astype(jnp.float32)
    selected = jnp.einsum('tke,ted->tkd', one_hot, pair_sum, precision=lax.Precision.HIGHEST)
    hot_expert = hot_index // (FFW // BLK)
    is_hot = (route_ids == hot_expert).astype(jnp.float32)[:, :, None]
    routed_sum = lax.optimization_barrier(jnp.sum(gate_weights[:, :, None] * (selected + is_hot * hot_part[:, None, :]), axis=1))
    return (rows_float + routed_sum).astype(jnp.bfloat16)

def layer_load(route_layer, hot_index):
    member = (route_layer[..., None] == jnp.arange(EXPERTS, dtype=jnp.int32)).astype(jnp.int32)
    expert_total = lax.optimization_barrier(jnp.sum(member, axis=(0, 1, 2)))
    device_ids = jnp.arange(N_EP, dtype=jnp.int32)
    home_units = expert_total[device_ids // 2] * (2 - (device_ids == hot_index // 2).astype(jnp.int32))
    hot_expert = hot_index // (FFW // BLK)
    per_token = lax.optimization_barrier(jnp.sum((route_layer == hot_expert).astype(jnp.int32), axis=(0, 2)))
    own_units = lax.optimization_barrier(jnp.sum(per_token.reshape(N_EP, TOK_DEV), axis=1))
    unit_count = (home_units + own_units).astype(jnp.float32)
    return unit_count / float(MICRO * TOK_DEV * TOP * (FFW // BLK))

def reference(rows_in, routes, hot_blocks, gains, router, w_gate, w_up, w_down):
    current = rows_in
    layer_rows = []
    load_rows = []
    for layer_index in range(LAYERS):
        down_float = w_down[layer_index].astype(jnp.float32).reshape(N_EP, 2 * BLK, D)
        hot_index = hot_blocks[layer_index]
        next_list = []
        for micro_index in range(MICRO):
            next_list.append(apply_layer(current[micro_index], routes[layer_index, micro_index], hot_index, gains[layer_index], router[layer_index], w_gate[layer_index], w_up[layer_index], w_down[layer_index], down_float))
        current = jnp.stack(next_list)
        layer_rows.append(current)
        load_rows.append(layer_load(routes[layer_index], hot_index))
    return (jnp.stack(layer_rows), jnp.stack(load_rows))
```

```python
import jax
import jax.numpy as jnp
from jax import lax
from jax.sharding import PartitionSpec as P

FFW = 1024
BLK = 256


def shifted(block, axis, distance):
    devices = range(lax.axis_size(axis))
    route = [(i - distance, i) for i in devices if i - distance in devices]
    return lax.ppermute(block, axis, route)


def local(rows_in, routes, hot_blocks, gains, router, w_gate, w_up, w_down):
    section_index = lax.axis_index("section")
    ep_index = lax.axis_index("ep")
    section_count = lax.axis_size("section")
    micro_count = rows_in.shape[0]
    tok_rows = rows_in.shape[1]
    model_width = rows_in.shape[2]
    expert_count = router.shape[2]
    top_count = routes.shape[3]
    capacity = tok_rows // 2
    blocks_per_expert = FFW // BLK
    hot_index = hot_blocks[0]
    owner_index = hot_index // 2
    hot_expert = hot_index // blocks_per_expert
    norm_gain = gains[0]
    router_w = router[0]
    gate_w = w_gate[0]
    up_w = w_up[0]
    down_w = w_down[0]
    expert_ids = lax.iota(jnp.int32, expert_count)

    route_member = (routes[0][..., None] == expert_ids).astype(jnp.float32)
    expert_local = jnp.sum(route_member, axis=(0, 1, 2))
    expert_total = lax.psum(expert_local, "ep")
    own_expert = ep_index // 2
    home_units = jnp.sum(jnp.where(expert_ids == own_expert, expert_total, 0.0))
    own_hot = jnp.sum(jnp.where(expert_ids == hot_expert, expert_local, 0.0))

    def expert_rows(flat_rows):
        gate_value = jnp.dot(flat_rows, gate_w, preferred_element_type=jnp.float32)
        up_value = jnp.dot(flat_rows, up_w, preferred_element_type=jnp.float32)
        activation = (jax.nn.silu(gate_value) * up_value).astype(jnp.bfloat16)
        return jnp.dot(activation, down_w, preferred_element_type=jnp.float32).astype(jnp.bfloat16)

    def apply_layer(layer_input, route_ids):
        rows_float = layer_input.astype(jnp.float32)
        mean_square = jnp.mean(rows_float * rows_float, axis=-1, keepdims=True)
        normed = (rows_float * lax.rsqrt(mean_square + 1e-06) * norm_gain).astype(jnp.bfloat16)
        scores = jax.nn.sigmoid(jnp.dot(normed, router_w, preferred_element_type=jnp.float32))
        member = (route_ids[:, :, None] == expert_ids[None, None, :]).astype(jnp.float32)
        chosen = jnp.sum(member * scores[:, None, :], axis=2)
        gate_weights = 2.5 * chosen / jnp.sum(chosen, axis=1, keepdims=True)
        token_gate = jnp.sum(member * gate_weights[:, :, None], axis=1)
        routed = jnp.sum(member, axis=1)
        slot_rank = jnp.cumsum(routed, axis=0) - routed
        slot_ids = lax.iota(jnp.float32, capacity)
        placement = routed.T[:, None, :] * (
            slot_rank.T[:, None, :] == slot_ids[None, :, None]
        ).astype(jnp.float32)
        packed = jnp.einsum(
            "ect,tf->ecf",
            placement.astype(jnp.bfloat16),
            normed,
            preferred_element_type=jnp.float32,
        ).astype(jnp.bfloat16)
        send_rows = jnp.repeat(packed, 2, axis=0)
        recv_rows = lax.all_to_all(send_rows, "ep", split_axis=0, concat_axis=0, tiled=True)
        sources = recv_rows.shape[0]
        item_count = recv_rows.shape[1]
        part = expert_rows(recv_rows.reshape(sources * item_count, model_width))
        part = part.reshape(sources, item_count, model_width)
        home_back = lax.all_to_all(part, "ep", split_axis=0, concat_axis=0, tiled=True)
        combined = home_back.astype(jnp.float32).reshape(expert_count, 2, capacity, model_width)
        pair_sum = combined[:, 0] + combined[:, 1]
        weighting = placement * token_gate.T[:, None, :]
        routed_sum = jnp.einsum("ect,ecf->tf", weighting, pair_sum, precision=lax.Precision.HIGHEST)
        return (rows_float + routed_sum).astype(jnp.bfloat16)

    def run_tick(tick_index, loop_state):
        incoming, outputs = loop_state
        micro_index = tick_index - section_index
        is_live = (micro_index >= 0) & (micro_index < micro_count)
        clipped = jnp.clip(micro_index, 0, micro_count - 1)
        fresh_rows = lax.dynamic_index_in_dim(rows_in, clipped, 0, keepdims=False)
        layer_input = jnp.where(section_index == 0, fresh_rows, incoming)
        route_ids = lax.dynamic_index_in_dim(routes[0], clipped, 0, keepdims=False)
        next_rows = apply_layer(layer_input, route_ids)
        updated = lax.dynamic_update_index_in_dim(outputs, next_rows, clipped, 0)
        outputs = jnp.where(is_live, updated, outputs)
        incoming = shifted(next_rows, "section", 1)
        return (incoming, outputs)

    tick_count = micro_count + section_count - 1
    start_state = (
        jnp.zeros((tok_rows, model_width), jnp.bfloat16),
        jnp.zeros(rows_in.shape, jnp.bfloat16),
    )
    final_state = lax.fori_loop(0, tick_count, run_tick, start_state)
    outputs = final_state[1]
    unit_count = home_units * (2.0 - (owner_index == ep_index).astype(jnp.float32)) + own_hot
    relative = unit_count / float(micro_count * tok_rows * top_count * blocks_per_expert)
    return (outputs[None], relative.reshape(1, 1))


def solution(mesh):
    return jax.shard_map(
        local,
        mesh=mesh,
        in_specs=(
            P(None, "ep", None),
            P("section", None, "ep", None),
            P("section"),
            P("section", None),
            P("section", None, None),
            P("section", None, "ep"),
            P("section", None, "ep"),
            P("section", "ep", None),
        ),
        out_specs=(P("section", None, "ep", None), P("section", "ep")),
        check_vma=False,
    )
```

```python
import jax
import jax.numpy as jnp
from jax import lax
from jax.sharding import PartitionSpec as P

FFW = 1024
BLK = 256


def shifted(block, axis, distance):
    devices = range(lax.axis_size(axis))
    route = [(i - distance, i) for i in devices if i - distance in devices]
    return lax.ppermute(block, axis, route)


def local(rows_in, routes, hot_blocks, gains, router, w_gate, w_up, w_down):
    section_index = lax.axis_index("section")
    ep_index = lax.axis_index("ep")
    section_count = lax.axis_size("section")
    micro_count = rows_in.shape[0]
    tok_rows = rows_in.shape[1]
    model_width = rows_in.shape[2]
    expert_count = router.shape[2]
    top_count = routes.shape[3]
    capacity = tok_rows // 2
    blocks_per_expert = FFW // BLK
    hot_index = hot_blocks[0]
    owner_index = hot_index // 2
    hot_expert = hot_index // blocks_per_expert
    norm_gain = gains[0]
    router_w = router[0]
    gate_w = w_gate[0]
    up_w = w_up[0]
    down_w = w_down[0]
    expert_ids = lax.iota(jnp.int32, expert_count)

    route_member = (routes[0][..., None] == expert_ids).astype(jnp.float32)
    expert_local = jnp.sum(route_member, axis=(0, 1, 2))
    expert_total = lax.psum(expert_local, "ep")
    own_expert = ep_index // 2
    home_units = jnp.sum(jnp.where(expert_ids == own_expert, expert_total, 0.0))
    own_hot = jnp.sum(jnp.where(expert_ids == hot_expert, expert_local, 0.0))

    def expert_rows(flat_rows):
        gate_value = jnp.dot(flat_rows, gate_w, preferred_element_type=jnp.float32)
        up_value = jnp.dot(flat_rows, up_w, preferred_element_type=jnp.float32)
        activation = (jax.nn.silu(gate_value) * up_value).astype(jnp.bfloat16)
        return jnp.dot(activation, down_w, preferred_element_type=jnp.float32).astype(jnp.bfloat16)

    def apply_layer(layer_input, route_ids):
        rows_float = layer_input.astype(jnp.float32)
        mean_square = jnp.mean(rows_float * rows_float, axis=-1, keepdims=True)
        normed = (rows_float * lax.rsqrt(mean_square + 1e-06) * norm_gain).astype(jnp.bfloat16)
        scores = jax.nn.sigmoid(jnp.dot(normed, router_w, preferred_element_type=jnp.float32))
        member = (route_ids[..., None] == expert_ids).astype(jnp.float32)
        chosen = jnp.sum(member * scores[:, :, None, :], axis=3)
        gate_weights = 2.5 * chosen / jnp.sum(chosen, axis=2, keepdims=True)
        token_gate = jnp.sum(member * gate_weights[..., None], axis=2)
        routed = jnp.sum(member, axis=2)
        slot_rank = jnp.cumsum(routed, axis=1) - routed
        slot_ids = lax.iota(jnp.float32, capacity)
        placement = jnp.swapaxes(routed, 1, 2)[:, :, None, :] * (
            jnp.swapaxes(slot_rank, 1, 2)[:, :, None, :] == slot_ids[None, None, :, None]
        ).astype(jnp.float32)
        packed = jnp.einsum(
            "mect,mtf->emcf",
            placement.astype(jnp.bfloat16),
            normed,
            preferred_element_type=jnp.float32,
        ).astype(jnp.bfloat16)
        packed = packed.reshape(expert_count, micro_count * capacity, model_width)
        send_rows = jnp.repeat(packed, 2, axis=0)
        recv_rows = lax.all_to_all(send_rows, "ep", split_axis=0, concat_axis=0, tiled=True)
        sources = recv_rows.shape[0]
        item_count = recv_rows.shape[1]
        part = expert_rows(recv_rows.reshape(sources * item_count, model_width))
        part = part.reshape(sources, item_count, model_width)
        home_back = lax.all_to_all(part, "ep", split_axis=0, concat_axis=0, tiled=True)
        combined = home_back.astype(jnp.float32).reshape(
            expert_count, 2, micro_count, capacity, model_width
        )
        pair_sum = combined[:, 0] + combined[:, 1]
        weighting = placement * jnp.swapaxes(token_gate, 1, 2)[:, :, None, :]
        routed_sum = jnp.einsum(
            "mect,emcf->mtf", weighting, pair_sum, precision=lax.Precision.HIGHEST
        )
        return (rows_float + routed_sum).astype(jnp.bfloat16)

    route_ids = routes[0]

    def run_step(step, loop_state):
        incoming, outputs = loop_state
        layer_input = jnp.where(section_index == 0, rows_in, incoming)
        next_rows = apply_layer(layer_input, route_ids)
        outputs = jnp.where(section_index == step, next_rows, outputs)
        return (shifted(next_rows, "section", 1), outputs)

    start_state = (jnp.zeros(rows_in.shape, jnp.bfloat16), jnp.zeros(rows_in.shape, jnp.bfloat16))
    outputs = lax.fori_loop(0, section_count, run_step, start_state)[1]
    unit_count = home_units * (2.0 - (owner_index == ep_index).astype(jnp.float32)) + own_hot
    relative = unit_count / float(micro_count * tok_rows * top_count * blocks_per_expert)
    return (outputs[None], relative.reshape(1, 1))


def solution(mesh):
    return jax.shard_map(
        local,
        mesh=mesh,
        in_specs=(
            P(None, "ep", None),
            P("section", None, "ep", None),
            P("section"),
            P("section", None),
            P("section", None, None),
            P("section", None, "ep"),
            P("section", None, "ep"),
            P("section", "ep", None),
        ),
        out_specs=(P("section", None, "ep", None), P("section", "ep")),
        check_vma=False,
    )
```

```python
import jax
import jax.numpy as jnp
from jax import lax
from jax.sharding import PartitionSpec as P

FFW = 1024
BLK = 256


def shifted(block, axis, distance):
    devices = range(lax.axis_size(axis))
    route = [(i - distance, i) for i in devices if i - distance in devices]
    return lax.ppermute(block, axis, route)


def local(rows_in, routes, hot_blocks, gains, router, w_gate, w_up, w_down):
    section_index = lax.axis_index("section")
    ep_index = lax.axis_index("ep")
    section_count = lax.axis_size("section")
    micro_count = rows_in.shape[0]
    tok_rows = rows_in.shape[1]
    model_width = rows_in.shape[2]
    expert_count = router.shape[2]
    top_count = routes.shape[3]
    capacity = tok_rows // 2
    blocks_per_expert = FFW // BLK
    hot_index = hot_blocks[0]
    owner_index = hot_index // 2
    hot_expert = hot_index // blocks_per_expert
    norm_gain = gains[0]
    router_w = router[0]
    gate_w = w_gate[0]
    up_w = w_up[0]
    down_w = w_down[0]
    expert_ids = lax.iota(jnp.int32, expert_count)

    route_member = (routes[0][..., None] == expert_ids).astype(jnp.float32)
    expert_local = jnp.sum(route_member, axis=(0, 1, 2))
    expert_total = lax.psum(expert_local, "ep")
    own_expert = ep_index // 2
    home_units = jnp.sum(jnp.where(expert_ids == own_expert, expert_total, 0.0))
    own_hot = jnp.sum(jnp.where(expert_ids == hot_expert, expert_local, 0.0))

    def expert_rows(flat_rows):
        gate_value = jnp.dot(flat_rows, gate_w, preferred_element_type=jnp.float32)
        up_value = jnp.dot(flat_rows, up_w, preferred_element_type=jnp.float32)
        activation = (jax.nn.silu(gate_value) * up_value).astype(jnp.bfloat16)
        return jnp.dot(activation, down_w, preferred_element_type=jnp.float32).astype(jnp.bfloat16)

    def apply_layer(layer_input, route_ids):
        rows_float = layer_input.astype(jnp.float32)
        mean_square = jnp.mean(rows_float * rows_float, axis=-1, keepdims=True)
        normed = (rows_float * lax.rsqrt(mean_square + 1e-06) * norm_gain).astype(jnp.bfloat16)
        scores = jax.nn.sigmoid(jnp.dot(normed, router_w, preferred_element_type=jnp.float32))
        member = (route_ids[..., None] == expert_ids).astype(jnp.float32)
        chosen = jnp.sum(member * scores[:, :, None, :], axis=3)
        gate_weights = 2.5 * chosen / jnp.sum(chosen, axis=2, keepdims=True)
        token_gate = jnp.sum(member * gate_weights[..., None], axis=2)
        routed = jnp.sum(member, axis=2)
        slot_rank = jnp.cumsum(routed, axis=1) - routed
        slot_ids = lax.iota(jnp.float32, capacity)
        placement = jnp.swapaxes(routed, 1, 2)[:, :, None, :] * (
            jnp.swapaxes(slot_rank, 1, 2)[:, :, None, :] == slot_ids[None, None, :, None]
        ).astype(jnp.float32)
        packed = jnp.einsum(
            "mect,mtf->emcf",
            placement.astype(jnp.bfloat16),
            normed,
            preferred_element_type=jnp.float32,
        ).astype(jnp.bfloat16)
        packed = packed.reshape(expert_count, micro_count * capacity, model_width)
        send_rows = jnp.repeat(packed, 2, axis=0)
        recv_rows = lax.all_to_all(send_rows, "ep", split_axis=0, concat_axis=0, tiled=True)
        sources = recv_rows.shape[0]
        item_count = recv_rows.shape[1]
        part = expert_rows(recv_rows.reshape(sources * item_count, model_width))
        part = part.reshape(sources, item_count, model_width)
        home_back = lax.all_to_all(part, "ep", split_axis=0, concat_axis=0, tiled=True)
        combined = home_back.astype(jnp.float32).reshape(
            expert_count, 2, micro_count, capacity, model_width
        )
        pair_sum = combined[:, 0] + combined[:, 1]
        weighting = placement * jnp.swapaxes(token_gate, 1, 2)[:, :, None, :]
        routed_sum = jnp.einsum(
            "mect,emcf->mtf", weighting, pair_sum, precision=lax.Precision.HIGHEST
        )
        return (rows_float + routed_sum).astype(jnp.bfloat16)

    route_ids = routes[0]

    def run_step(step, loop_state):
        incoming, outputs = loop_state
        layer_input = jnp.where(section_index == 0, rows_in, incoming)
        next_rows = lax.cond(
            section_index == step,
            lambda rows: apply_layer(rows, route_ids),
            lambda rows: rows,
            layer_input,
        )
        outputs = jnp.where(section_index == step, next_rows, outputs)
        return (shifted(next_rows, "section", 1), outputs)

    start_state = (jnp.zeros(rows_in.shape, jnp.bfloat16), jnp.zeros(rows_in.shape, jnp.bfloat16))
    outputs = lax.fori_loop(0, section_count, run_step, start_state)[1]
    unit_count = home_units * (2.0 - (owner_index == ep_index).astype(jnp.float32)) + own_hot
    relative = unit_count / float(micro_count * tok_rows * top_count * blocks_per_expert)
    return (outputs[None], relative.reshape(1, 1))


def solution(mesh):
    return jax.shard_map(
        local,
        mesh=mesh,
        in_specs=(
            P(None, "ep", None),
            P("section", None, "ep", None),
            P("section"),
            P("section", None),
            P("section", None, None),
            P("section", None, "ep"),
            P("section", None, "ep"),
            P("section", "ep", None),
        ),
        out_specs=(P("section", None, "ep", None), P("section", "ep")),
        check_vma=False,
    )
```

```python
import jax
import jax.numpy as jnp
from jax import lax
from jax.sharding import PartitionSpec as P

FFW = 1024
BLK = 256


def shifted(block, axis, distance):
    devices = range(lax.axis_size(axis))
    route = [(i - distance, i) for i in devices if i - distance in devices]
    return lax.ppermute(block, axis, route)


def local(rows_in, routes, hot_blocks, gains, router, w_gate, w_up, w_down):
    section_index = lax.axis_index("section")
    ep_index = lax.axis_index("ep")
    section_count = lax.axis_size("section")
    micro_count = rows_in.shape[0]
    tok_rows = rows_in.shape[1]
    model_width = rows_in.shape[2]
    expert_count = router.shape[2]
    top_count = routes.shape[3]
    capacity = tok_rows // 2
    blocks_per_expert = FFW // BLK
    hot_index = hot_blocks[0]
    owner_index = hot_index // 2
    hot_expert = hot_index // blocks_per_expert
    norm_gain = gains[0]
    router_w = router[0]
    gate_w = w_gate[0]
    up_w = w_up[0]
    down_w = w_down[0]
    expert_ids = lax.iota(jnp.int32, expert_count)

    route_member = (routes[0][..., None] == expert_ids).astype(jnp.float32)
    expert_local = jnp.sum(route_member, axis=(0, 1, 2))
    own_hot = jnp.sum(jnp.where(expert_ids == hot_expert, expert_local, 0.0))

    def expert_rows(flat_rows):
        gate_value = jnp.dot(flat_rows, gate_w, preferred_element_type=jnp.float32)
        up_value = jnp.dot(flat_rows, up_w, preferred_element_type=jnp.float32)
        activation = (jax.nn.silu(gate_value) * up_value).astype(jnp.bfloat16)
        return jnp.dot(activation, down_w, preferred_element_type=jnp.float32).astype(jnp.bfloat16)

    def apply_layer(layer_input, route_ids):
        rows_float = layer_input.astype(jnp.float32)
        mean_square = jnp.mean(rows_float * rows_float, axis=-1, keepdims=True)
        normed = (rows_float * lax.rsqrt(mean_square + 1e-06) * norm_gain).astype(jnp.bfloat16)
        scores = jax.nn.sigmoid(jnp.dot(normed, router_w, preferred_element_type=jnp.float32))
        member = (route_ids[..., None] == expert_ids).astype(jnp.float32)
        chosen = jnp.sum(member * scores[:, :, None, :], axis=3)
        gate_weights = 2.5 * chosen / jnp.sum(chosen, axis=2, keepdims=True)
        token_gate = jnp.sum(member * gate_weights[..., None], axis=2)
        routed = jnp.sum(member, axis=2)
        slot_rank = jnp.cumsum(routed, axis=1) - routed
        slot_ids = lax.iota(jnp.float32, capacity)
        placement = jnp.swapaxes(routed, 1, 2)[:, :, None, :] * (
            jnp.swapaxes(slot_rank, 1, 2)[:, :, None, :] == slot_ids[None, None, :, None]
        ).astype(jnp.float32)
        packed = jnp.einsum(
            "mect,mtf->emcf",
            placement.astype(jnp.bfloat16),
            normed,
            preferred_element_type=jnp.float32,
        ).astype(jnp.bfloat16)
        item_count = micro_count * capacity
        packed = packed.reshape(expert_count, item_count, model_width)
        count_row = jnp.broadcast_to(
            jnp.sum(routed, axis=(0, 1))[:, None, None], (expert_count, 1, model_width)
        ).astype(jnp.bfloat16)
        send_rows = jnp.repeat(jnp.concatenate([packed, count_row], axis=1), 2, axis=0)
        recv_all = lax.all_to_all(send_rows, "ep", split_axis=0, concat_axis=0, tiled=True)
        recv_rows = recv_all[:, :item_count]
        filled = jnp.sum(recv_all[:, item_count, 0].astype(jnp.float32))
        sources = recv_rows.shape[0]
        part = expert_rows(recv_rows.reshape(sources * item_count, model_width))
        part = part.reshape(sources, item_count, model_width)
        home_back = lax.all_to_all(part, "ep", split_axis=0, concat_axis=0, tiled=True)
        combined = home_back.astype(jnp.float32).reshape(
            expert_count, 2, micro_count, capacity, model_width
        )
        pair_sum = combined[:, 0] + combined[:, 1]
        weighting = placement * jnp.swapaxes(token_gate, 1, 2)[:, :, None, :]
        routed_sum = jnp.einsum(
            "mect,emcf->mtf", weighting, pair_sum, precision=lax.Precision.HIGHEST
        )
        return ((rows_float + routed_sum).astype(jnp.bfloat16), filled)

    route_ids = routes[0]

    def run_step(step, loop_state):
        incoming, outputs, home_units = loop_state
        layer_input = jnp.where(section_index == 0, rows_in, incoming)
        next_rows, filled = lax.cond(
            section_index == step,
            lambda rows: apply_layer(rows, route_ids),
            lambda rows: (rows, jnp.float32(0.0)),
            layer_input,
        )
        outputs = jnp.where(section_index == step, next_rows, outputs)
        return (shifted(next_rows, "section", 1), outputs, home_units + filled)

    start_state = (
        jnp.zeros(rows_in.shape, jnp.bfloat16),
        jnp.zeros(rows_in.shape, jnp.bfloat16),
        jnp.float32(0.0),
    )
    _, outputs, home_units = lax.fori_loop(0, section_count, run_step, start_state)
    unit_count = home_units * (2.0 - (owner_index == ep_index).astype(jnp.float32)) + own_hot
    relative = unit_count / float(micro_count * tok_rows * top_count * blocks_per_expert)
    return (outputs[None], relative.reshape(1, 1))


def solution(mesh):
    return jax.shard_map(
        local,
        mesh=mesh,
        in_specs=(
            P(None, "ep", None),
            P("section", None, "ep", None),
            P("section"),
            P("section", None),
            P("section", None, None),
            P("section", None, "ep"),
            P("section", None, "ep"),
            P("section", "ep", None),
        ),
        out_specs=(P("section", None, "ep", None), P("section", "ep")),
        check_vma=False,
    )
```

```python
import jax
import jax.numpy as jnp
from jax import lax
from jax.sharding import PartitionSpec as P

FFW = 1024
BLK = 256


def shifted(block, axis, distance):
    devices = range(lax.axis_size(axis))
    route = [(i - distance, i) for i in devices if i - distance in devices]
    return lax.ppermute(block, axis, route)


def local(rows_in, routes, hot_blocks, gains, router, w_gate, w_up, w_down):
    section_index = lax.axis_index("section")
    ep_index = lax.axis_index("ep")
    section_count = lax.axis_size("section")
    micro_count = rows_in.shape[0]
    tok_rows = rows_in.shape[1]
    model_width = rows_in.shape[2]
    expert_count = router.shape[2]
    top_count = routes.shape[3]
    capacity = tok_rows // 2
    blocks_per_expert = FFW // BLK
    hot_index = hot_blocks[0]
    owner_index = hot_index // 2
    hot_expert = hot_index // blocks_per_expert
    norm_gain = gains[0]
    router_w = router[0]
    gate_w = w_gate[0]
    up_w = w_up[0]
    down_w = w_down[0]
    expert_ids = lax.iota(jnp.int32, expert_count)

    route_member = (routes[0][..., None] == expert_ids).astype(jnp.float32)
    expert_local = jnp.sum(route_member, axis=(0, 1, 2))
    own_expert = ep_index // 2
    own_hot = jnp.sum(jnp.where(expert_ids == hot_expert, expert_local, 0.0))

    def expert_rows(flat_rows):
        gate_value = jnp.dot(flat_rows, gate_w, preferred_element_type=jnp.float32)
        up_value = jnp.dot(flat_rows, up_w, preferred_element_type=jnp.float32)
        activation = (jax.nn.silu(gate_value) * up_value).astype(jnp.bfloat16)
        return jnp.dot(activation, down_w, preferred_element_type=jnp.float32).astype(jnp.bfloat16)

    def apply_layer(layer_input, route_ids):
        rows_float = layer_input.astype(jnp.float32)
        mean_square = jnp.mean(rows_float * rows_float, axis=-1, keepdims=True)
        normed = (rows_float * lax.rsqrt(mean_square + 1e-06) * norm_gain).astype(jnp.bfloat16)
        scores = jax.nn.sigmoid(jnp.dot(normed, router_w, preferred_element_type=jnp.float32))
        member = (route_ids[..., None] == expert_ids).astype(jnp.float32)
        chosen = jnp.sum(member * scores[:, :, None, :], axis=3)
        gate_weights = 2.5 * chosen / jnp.sum(chosen, axis=2, keepdims=True)
        token_gate = jnp.sum(member * gate_weights[..., None], axis=2)
        routed = jnp.sum(member, axis=2)
        slot_rank = jnp.cumsum(routed, axis=1) - routed
        slot_ids = lax.iota(jnp.float32, capacity)
        placement = jnp.swapaxes(routed, 1, 2)[:, :, None, :] * (
            jnp.swapaxes(slot_rank, 1, 2)[:, :, None, :] == slot_ids[None, None, :, None]
        ).astype(jnp.float32)
        packed = jnp.einsum(
            "mect,mtf->emcf",
            placement.astype(jnp.bfloat16),
            normed,
            preferred_element_type=jnp.float32,
        ).astype(jnp.bfloat16)
        packed = packed.reshape(expert_count, micro_count * capacity, model_width)
        send_rows = jnp.repeat(packed, 2, axis=0)
        recv_rows = lax.all_to_all(send_rows, "ep", split_axis=0, concat_axis=0, tiled=True)
        sources = recv_rows.shape[0]
        item_count = recv_rows.shape[1]
        part = expert_rows(recv_rows.reshape(sources * item_count, model_width))
        part = part.reshape(sources, item_count, model_width)
        home_back = lax.all_to_all(part, "ep", split_axis=0, concat_axis=0, tiled=True)
        combined = home_back.astype(jnp.float32).reshape(
            expert_count, 2, micro_count, capacity, model_width
        )
        pair_sum = combined[:, 0] + combined[:, 1]
        weighting = placement * jnp.swapaxes(token_gate, 1, 2)[:, :, None, :]
        routed_sum = jnp.einsum(
            "mect,emcf->mtf", weighting, pair_sum, precision=lax.Precision.HIGHEST
        )
        expert_total = lax.psum(expert_local, "ep")
        filled = jnp.sum(jnp.where(expert_ids == own_expert, expert_total, 0.0))
        return ((rows_float + routed_sum).astype(jnp.bfloat16), filled)

    route_ids = routes[0]

    def run_step(step, loop_state):
        incoming, outputs, home_units = loop_state
        layer_input = jnp.where(section_index == 0, rows_in, incoming)
        next_rows, filled = lax.cond(
            section_index == step,
            lambda rows: apply_layer(rows, route_ids),
            lambda rows: (rows, jnp.float32(0.0)),
            layer_input,
        )
        outputs = jnp.where(section_index == step, next_rows, outputs)
        return (shifted(next_rows, "section", 1), outputs, home_units + filled)

    start_state = (
        jnp.zeros(rows_in.shape, jnp.bfloat16),
        jnp.zeros(rows_in.shape, jnp.bfloat16),
        jnp.float32(0.0),
    )
    _, outputs, home_units = lax.fori_loop(0, section_count, run_step, start_state)
    unit_count = home_units * (2.0 - (owner_index == ep_index).astype(jnp.float32)) + own_hot
    relative = unit_count / float(micro_count * tok_rows * top_count * blocks_per_expert)
    return (outputs[None], relative.reshape(1, 1))


def solution(mesh):
    return jax.shard_map(
        local,
        mesh=mesh,
        in_specs=(
            P(None, "ep", None),
            P("section", None, "ep", None),
            P("section"),
            P("section", None),
            P("section", None, None),
            P("section", None, "ep"),
            P("section", None, "ep"),
            P("section", "ep", None),
        ),
        out_specs=(P("section", None, "ep", None), P("section", "ep")),
        check_vma=False,
    )
```
